32 devices in a mesh: pair: 16 (over z, x, core), virt: 2 (over y).
Axes of the slice: x: 2, y: 2, z: 4, core: 2. Of those that a mesh axis runs over, the one named last changes fastest.
Arguments:
- amplitudes: bfloat16 [96, 96, 128, 128], P('pair', None, 'virt'), may hold values from -6 to 6
- integrals: bfloat16 [128, 20, 128, 128], P('virt'), may hold values from -0.125 to 0.125
- cd_tiles: int32 [128, 20], P('virt'), may hold values from 0 to 127, as said below
- tile_counts: int32 [128], P('virt'), may hold values from 10 to 20, as said below
- eps_occ: float32 [96], replicated, may hold values from -2 to -0.5
- eps_virt: float32 [128], replicated, may hold values from 0.5 to 3
Outputs:
- new_amplitudes: bfloat16 [96, 96, 128, 128], P('pair', None, 'virt')
The draws below stay inside these ranges and needn't reach their ends.
Inputs may be any that keep to these rules, and one draw needn't show every extreme that they name: `cd_tiles`: row a holds 20 different numbers from lo(a) to lo(a) + 2 * 64 - 1, where lo(a) = min(max(a - 64, 0), 0); only its first tile_counts[a] entries are live. `tile_counts`: some entry equals 20.
All inputs are finite; a program needn't handle non-finite values.
Results may differ from the reference program's by a relative error of at most 0.001.
Values may be sent and summed in bfloat16 or wider, within the bound.
A program may use at most 448 MiB of HBM per device.

```python
import jax
import jax.numpy as jnp
from jax import lax

O = 96
NVW = 128
CAP = 20
A_DEV = 64


def tile_table(key):
    base = jax.random.fold_in(key, 1234)
    first, second, third = jax.random.split(base, 3)
    counts = jax.random.randint(first, (NVW,), CAP - CAP // 2, CAP + 1)
    position = jax.random.randint(second, (), 0, NVW)
    positions = jnp.arange(NVW, dtype=jnp.int32)
    counts = jnp.where(positions == position, CAP, counts).astype(jnp.int32)
    lowest = jnp.clip(positions - A_DEV, 0, NVW - 2 * A_DEV)
    row_keys = jax.random.split(third, NVW)

    def permute_row(row_key):
        return jax.random.permutation(row_key, 2 * A_DEV)
    orders = jax.vmap(permute_row)(row_keys)
    tile_list = lowest[:, None] + orders[:, :CAP]
    return (tile_list.astype(jnp.int32), counts)


def draw_cd_tiles(key, part):
    return tile_table(key)[0]


def draw_tile_counts(key, part):
    return tile_table(key)[1]


def block_levels(stream_key, shape, cuts, low, high):
    factor_of, own = 1.0, jax.random.fold_in(stream_key, 6)
    for dim, blocks in cuts:
        steps = jnp.exp(jax.random.uniform(jax.random.fold_in(own, dim), (blocks,), jnp.float32, low / len(cuts), high / len(cuts)))
        factor_of = factor_of * jnp.repeat(steps, shape[dim] // blocks).reshape([-1 if axis == dim else 1 for axis in range(len(shape))])
    return factor_of


def scatter_about(key, dims, deviation, reach, shards=(), kind=jnp.bfloat16):
    drawn = jax.random.normal(key, dims, jnp.float32) * deviation
    if len(shards) > 0:
        drawn = block_levels(key, dims, shards, -0.22, 0.18) * drawn
    return jnp.clip(drawn, min=-reach, max=reach).astype(kind)


def setup_inputs(seed: int = 0) -> dict:
    streams_of = jax.random.split(jax.random.key(seed), 7)
    return {
        "amplitudes": scatter_about(streams_of[0], (O, O, NVW, NVW), 1.0, 6.0, ((0, 16), (2, 2))),
        "integrals": scatter_about(streams_of[1], (NVW, CAP, NVW, NVW), (CAP * NVW) ** -0.5, 0.125, ((0, 2),)),
        "cd_tiles": draw_cd_tiles(jax.random.fold_in(streams_of[6], 71), 0),
        "tile_counts": draw_tile_counts(jax.random.fold_in(streams_of[6], 71), 0),
        "eps_occ": jnp.clip(jax.random.uniform(streams_of[4], (O,), jnp.float32, -2.0, -0.5), -2.0, -0.5),
        "eps_virt": jnp.clip(jax.random.uniform(streams_of[5], (NVW,), jnp.float32, 0.5, 3.0), 0.5, 3.0),
    }


def reference(amplitudes, integrals, cd_tiles, tile_counts, eps_occ, eps_virt):
    slot_ids = jnp.arange(CAP, dtype=jnp.int32)
    live_slots = (slot_ids[None, :] < tile_counts[:, None]).astype(jnp.float32)

    def one_column(operands):
        tile_list, weights, kept = operands
        picked = jnp.take(amplitudes, tile_list.astype(jnp.int32), axis=2).astype(jnp.float32)
        masked = weights.astype(jnp.float32) * kept[:, None, None]
        return jnp.einsum("ijsd,sdb->ijb", picked, masked)

    ladder = lax.map(one_column, (cd_tiles, integrals, live_slots))
    ladder = jnp.transpose(ladder, (1, 2, 0, 3))
    symmetric = ladder + jnp.transpose(ladder, (1, 0, 3, 2))
    denominator = (eps_occ[:, None, None, None] + eps_occ[None, :, None, None]
                   - eps_virt[None, None, :, None] - eps_virt[None, None, None, :])
    return (symmetric / denominator).astype(jnp.bfloat16)
```

```python
import functools

import jax
import jax.numpy as jnp
from jax import lax
from jax.experimental import pallas as pl
from jax.experimental.pallas import tpu as pltpu
from jax.sharding import PartitionSpec as P

MESH = pl.DeviceIdType.MESH
STEP = 8
TOP = 32767.0


def extended(cells, sides, width):
    for axis, dim in sides:
        count = lax.axis_size(axis)
        ends = count - 1
        head = lax.slice_in_dim(cells, 0, width, axis=dim)
        tail = lax.slice_in_dim(cells, cells.shape[dim] - width, cells.shape[dim], axis=dim)
        cells = jnp.concatenate(
            [
                lax.ppermute(tail, axis, [(i, (i + 1) % count) for i in range(ends)]),
                cells,
                lax.ppermute(head, axis, [((i + 1) % count, i) for i in range(ends)]),
            ],
            axis=dim,
        )
    return cells


def general_device(amplitudes, integrals, cd_tiles, tile_counts, eps_occ, eps_virt):
    own_rows = amplitudes.shape[0]
    own_tiles = amplitudes.shape[2]
    slot_count = integrals.shape[1]
    first_tile = lax.axis_index("virt") * own_tiles
    first_row = lax.axis_index("pair") * own_rows
    local_tiles = cd_tiles - first_tile + own_tiles
    slot_ids = lax.broadcasted_iota(jnp.int32, cd_tiles.shape, 1)
    kept_slots = (slot_ids < tile_counts[:, None]).astype(jnp.bfloat16)
    masked_weights = integrals * kept_slots[:, :, None, None]
    padded = extended(amplitudes, (("virt", 2),), own_tiles)
    block_width = min(4, slot_count)
    ladder = None
    for block_start in range(0, slot_count, block_width):
        block_stop = min(block_start + block_width, slot_count)
        columns = local_tiles[:, block_start:block_stop]
        picked = jnp.take(padded, columns, axis=2)
        weights = masked_weights[:, block_start:block_stop]
        term = jnp.einsum("ijasd,asdb->ijab", picked, weights, preferred_element_type=jnp.float32)
        ladder = term if ladder is None else ladder + term
    arrived_ladder = lax.all_to_all(
        lax.all_to_all(ladder, "pair", split_axis=1, concat_axis=0, tiled=True),
        "virt",
        split_axis=3,
        concat_axis=2,
        tiled=True,
    )
    partner = jnp.transpose(arrived_ladder, (1, 0, 3, 2))
    occupied_own = lax.dynamic_slice_in_dim(eps_occ, first_row, own_rows)
    virtual_own = lax.dynamic_slice_in_dim(eps_virt, first_tile, own_tiles)
    denominator = (
        occupied_own[:, None, None, None]
        + eps_occ[None, :, None, None]
        - virtual_own[None, None, :, None]
        - eps_virt[None, None, None, :]
    )
    return ((ladder + partner) / denominator).astype(jnp.bfloat16)


def greet_all(pairs, virts):
    count = pairs * virts
    me = lax.axis_index("pair") * virts + lax.axis_index("virt")
    barrier = pltpu.get_barrier_semaphore()

    def greet(d, _):
        t = lax.rem(me + d, count)
        pl.semaphore_signal(
            barrier, inc=1, device_id=(t // virts, lax.rem(t, virts)), device_id_type=MESH
        )
        return 0

    lax.fori_loop(1, count, greet, 0)
    pl.semaphore_wait(barrier, count - 1)


def turn_tiles(block, picked, first):
    tall, held = block.shape[0], block.shape[1]

    def turn(x, _):
        rows = pl.ds(pl.multiple_of(x * 16, 16), 16)
        for c in range(0, held, 16):
            picked[pl.ds(first + c, 16), rows, :] = jnp.swapaxes(block[rows, pl.ds(c, 16), :], 0, 1)
        return 0

    lax.fori_loop(0, tall // 16, turn, 0)


def pack(pairs, mine, codes, scales):
    held, wide = codes.shape[2], codes.shape[3]
    duos = codes.shape[1]
    half = wide // 2
    low = lax.broadcasted_iota(jnp.int32, (held, wide), 1) < half
    low_row = low[:1]

    def one(p, _):
        for m in range(duos):
            tiles, sizes = [], []
            for e in range(2):
                spot = pl.ds(pl.multiple_of((p * 2 * duos + 2 * m + e) * held, 8), held)
                tile = mine[spot, :]
                top = jnp.maximum(jnp.max(jnp.abs(tile), axis=0, keepdims=True), 1e-30)
                tiles.append(jnp.round(tile * (TOP / top)))
                sizes.append(top / TOP)
            for v in range(2):
                moved = [
                    x if v == e else pltpu.roll(x, half, 1) for e, x in enumerate(tiles)
                ]
                code = jnp.where(low, moved[0], moved[1])
                codes[2 * p + v, m] = code.astype(jnp.int32).astype(jnp.int16)
                turned = [
                    x if v == e else pltpu.roll(x, half, 1) for e, x in enumerate(sizes)
                ]
                scales[2 * p + v, pl.ds(m, 1), :] = jnp.where(low_row, turned[0], turned[1])
        return 0

    lax.fori_loop(0, pairs, one, 0)


def fused_kernel(pairs, virts, *refs):
    tiles, occ_own, occ_all, amplitudes, weights, virt_own, virt_all = refs[:7]
    out, codes_far, scales_far = refs[7:10]
    own, other, picked, ladder, codes, scales, arrived, sizes, results = refs[10:19]
    own_sem, swap_send, swap_recv, hop, send, recv, send_s, recv_s, out_sem = refs[19:]
    r, k = pl.program_id(0), pl.program_id(1)
    rows, steps = pl.num_programs(0), pl.num_programs(1)
    chunks, others, held, depth = amplitudes.shape
    block, slots, _, wide = weights.shape
    count = pairs * virts
    p, v = lax.axis_index("pair"), lax.axis_index("virt")
    me = p * virts + v
    duos = codes.shape[1]

    def own_copy(x):
        return pltpu.make_async_copy(amplitudes.at[x], own, own_sem)

    def swap(x):
        return pltpu.make_async_remote_copy(
            src_ref=amplitudes.at[x],
            dst_ref=other.at[x],
            send_sem=swap_send.at[x],
            recv_sem=swap_recv.at[x],
            device_id=(p, 1 - v),
            device_id_type=MESH,
        )

    def moves(x, d):
        t = lax.rem(me + d, count)
        target = (t // virts, lax.rem(t, virts))
        return [
            pltpu.make_async_remote_copy(
                src_ref=source.at[x, t],
                dst_ref=land.at[x, me],
                send_sem=sent.at[x],
                recv_sem=got.at[x],
                device_id=target,
                device_id_type=MESH,
            )
            for source, land, sent, got in (
                (codes_far, arrived, send, recv),
                (scales_far, sizes, send_s, recv_s),
            )
        ]

    @pl.when((r == 0) & (k == 0))
    def _():
        own_copy(0).start()
        greet_all(pairs, virts)
        for x in range(chunks):
            swap(x).start()
        picked[2 * held] = jnp.zeros((others, depth), picked.dtype)

    @pl.when(k == 0)
    def _():
        own_copy(r).wait()
        turn_tiles(own, picked, 0)
        swap(r).wait_recv()
        turn_tiles(other.at[r], picked, held)

        @pl.when(r + 1 < rows)
        def _():
            own_copy(r + 1).start()

    for s in range(block):
        a = k * block + s
        lhs = jnp.concatenate([picked[tiles[a, x]] for x in range(slots)], axis=1)
        ladder[r, pl.ds(a, others, stride=held), :] = jnp.dot(
            lhs, weights[s].reshape(slots * depth, wide), preferred_element_type=jnp.float32
        )

    @pl.when(k == steps - 1)
    def _():
        pack(pairs, ladder.at[r], codes, scales)
        hops = (
            pltpu.make_async_copy(codes, codes_far.at[r], hop.at[0]),
            pltpu.make_async_copy(scales, scales_far.at[r], hop.at[1]),
        )
        for copy in hops:
            copy.start()
        for copy in hops:
            copy.wait()

        def begin(d, _):
            for copy in moves(r, d):
                copy.start()
            return 0

        lax.fori_loop(1, count, begin, 0)
        pltpu.make_async_copy(codes_far.at[r, me], arrived.at[r, me], recv.at[r]).start()
        pltpu.make_async_copy(scales_far.at[r, me], sizes.at[r, me], recv_s.at[r]).start()

    @pl.when((r == rows - 1) & (k == steps - 1))
    def _():
        low = virt_own[...] + virt_all[...]

        def result(n):
            slot = lax.rem(n, 2)
            j = lax.rem(n, pairs) * chunks + n // pairs
            return pltpu.make_async_copy(results.at[slot], out.at[:, j], out_sem.at[slot])

        def combine(n, _):
            c, q = n // pairs, lax.rem(n, pairs)
            slot = lax.rem(n, 2)

            @pl.when(q == 0)
            def _():
                pltpu.make_async_copy(arrived.at[c], arrived.at[c], recv.at[c]).wait()
                pltpu.make_async_copy(sizes.at[c], sizes.at[c], recv_s.at[c]).wait()

            @pl.when(n >= 2)
            def _():
                result(n - 2).wait()

            j = q * chunks + c
            for m in range(duos):
                tile = jnp.concatenate(
                    [
                        arrived[c, 2 * q + x, m].astype(jnp.float32)
                        * sizes[c, 2 * q + x, pl.ds(m, 1), :]
                        for x in range(virts)
                    ],
                    axis=0,
                )
                turned = tile.T
                for e in range(2):
                    i = 2 * m + e
                    mine = ladder[i, pl.ds(pl.multiple_of(j * held, 8), held), :]
                    level = occ_own[i] + occ_all[j]
                    partner = turned[e * held : (e + 1) * held]
                    results[slot, i] = ((mine + partner) / (level - low)).astype(results.dtype)
            result(n).start()
            return 0

        total = chunks * pairs
        lax.fori_loop(0, total, combine, 0)
        result(total - 2).wait()
        result(total - 1).wait()
        for x in range(chunks):
            swap(x).wait_send()
            most = pl.ds(0, count - 1)
            pltpu.make_async_copy(codes_far.at[x, most], codes_far.at[x, most], send.at[x]).wait()
            pltpu.make_async_copy(scales_far.at[x, most], scales_far.at[x, most], send_s.at[x]).wait()


def per_device(amplitudes, integrals, cd_tiles, tile_counts, eps_occ, eps_virt):
    pairs, virts = lax.axis_size("pair"), lax.axis_size("virt")
    rows, others, held, depth = amplitudes.shape
    slots, wide = integrals.shape[1], integrals.shape[3]
    fits = virts == 2 and held % 16 == 0 and rows % 2 == 0 and rows <= 16 and others % 16 == 0
    fits = fits and wide == 2 * held and wide == 128 and held % STEP == 0
    if not fits:
        return general_device(amplitudes, integrals, cd_tiles, tile_counts, eps_occ, eps_virt)
    count = pairs * virts
    duos = rows // 2
    steps = held // STEP
    first_tile = lax.axis_index("virt") * held
    first_row = lax.axis_index("pair") * rows
    slot_ids = lax.broadcasted_iota(jnp.int32, cd_tiles.shape, 1)
    places = lax.rem(cd_tiles - first_tile + 2 * held, 2 * held)
    tiles = jnp.where(slot_ids < tile_counts[:, None], places, 2 * held)
    occ_own = lax.dynamic_slice_in_dim(eps_occ, first_row, rows)
    virt_own = lax.dynamic_slice_in_dim(eps_virt, first_tile, held)
    anywhere = pl.BlockSpec(memory_space=pl.ANY)
    vmem = pl.BlockSpec(memory_space=pltpu.VMEM)
    code_shape = (count, duos, held, wide)
    scale_shape = (count, 8, wide)
    flops = 2 * rows * others * held * slots * depth * wide
    out, _, _ = pl.pallas_call(
        functools.partial(fused_kernel, pairs, virts),
        grid_spec=pltpu.PrefetchScalarGridSpec(
            num_scalar_prefetch=3,
            grid=(rows, steps),
            in_specs=[
                anywhere,
                pl.BlockSpec((STEP, slots, depth, wide), lambda r, k, *_: (k, 0, 0, 0)),
                vmem,
                vmem,
            ],
            out_specs=[anywhere] * 3,
            scratch_shapes=[
                pltpu.VMEM((others, held, depth), amplitudes.dtype),
                pltpu.VMEM((rows, others, held, depth), amplitudes.dtype),
                pltpu.VMEM((2 * held + 1, others, depth), amplitudes.dtype),
                pltpu.VMEM((rows, others * held, wide), jnp.float32),
                pltpu.VMEM(code_shape, jnp.int16),
                pltpu.VMEM(scale_shape, jnp.float32),
                pltpu.VMEM((rows,) + code_shape, jnp.int16),
                pltpu.VMEM((rows,) + scale_shape, jnp.float32),
                pltpu.VMEM((2, rows, held, wide), jnp.bfloat16),
                pltpu.SemaphoreType.DMA,
                pltpu.SemaphoreType.DMA((rows,)),
                pltpu.SemaphoreType.DMA((rows,)),
                pltpu.SemaphoreType.DMA((2,)),
                pltpu.SemaphoreType.DMA((rows,)),
                pltpu.SemaphoreType.DMA((rows,)),
                pltpu.SemaphoreType.DMA((rows,)),
                pltpu.SemaphoreType.DMA((rows,)),
                pltpu.SemaphoreType.DMA((2,)),
            ],
        ),
        out_shape=[
            jax.ShapeDtypeStruct(amplitudes.shape[:3] + (wide,), jnp.bfloat16),
            jax.ShapeDtypeStruct((rows,) + code_shape, jnp.int16),
            jax.ShapeDtypeStruct((rows,) + scale_shape, jnp.float32),
        ],
        cost_estimate=pl.CostEstimate(
            flops=flops, bytes_accessed=2 * rows * integrals.size, transcendentals=0
        ),
        compiler_params=pltpu.CompilerParams(
            vmem_limit_bytes=63 * 2**20, collective_id=0, has_side_effects=True
        ),
        name="ladder",
    )(
        tiles,
        occ_own,
        eps_occ,
        amplitudes,
        integrals,
        jnp.broadcast_to(virt_own[:, None], (held, wide)),
        jnp.broadcast_to(eps_virt[None, :], (held, wide)),
    )
    return out


def solution(mesh):
    in_specs = (
        P("pair", None, "virt", None),
        P("virt", None, None, None),
        P("virt", None),
        P("virt"),
        P(),
        P(),
    )
    out_specs = P("pair", None, "virt", None)
    return jax.shard_map(
        per_device, mesh=mesh, in_specs=in_specs, out_specs=out_specs, check_vma=False
    )
```

```python
import functools

import jax
import jax.numpy as jnp
from jax import lax
from jax.experimental import pallas as pl
from jax.experimental.pallas import tpu as pltpu
from jax.sharding import PartitionSpec as P

MESH = pl.DeviceIdType.MESH
STEP = 8
TOP = 32767.0


def extended(cells, sides, width):
    for axis, dim in sides:
        count = lax.axis_size(axis)
        ends = count - 1
        head = lax.slice_in_dim(cells, 0, width, axis=dim)
        tail = lax.slice_in_dim(cells, cells.shape[dim] - width, cells.shape[dim], axis=dim)
        cells = jnp.concatenate(
            [
                lax.ppermute(tail, axis, [(i, (i + 1) % count) for i in range(ends)]),
                cells,
                lax.ppermute(head, axis, [((i + 1) % count, i) for i in range(ends)]),
            ],
            axis=dim,
        )
    return cells


def general_device(amplitudes, integrals, cd_tiles, tile_counts, eps_occ, eps_virt):
    own_rows = amplitudes.shape[0]
    own_tiles = amplitudes.shape[2]
    slot_count = integrals.shape[1]
    first_tile = lax.axis_index("virt") * own_tiles
    first_row = lax.axis_index("pair") * own_rows
    local_tiles = cd_tiles - first_tile + own_tiles
    slot_ids = lax.broadcasted_iota(jnp.int32, cd_tiles.shape, 1)
    kept_slots = (slot_ids < tile_counts[:, None]).astype(jnp.bfloat16)
    masked_weights = integrals * kept_slots[:, :, None, None]
    padded = extended(amplitudes, (("virt", 2),), own_tiles)
    block_width = min(4, slot_count)
    ladder = None
    for block_start in range(0, slot_count, block_width):
        block_stop = min(block_start + block_width, slot_count)
        columns = local_tiles[:, block_start:block_stop]
        picked = jnp.take(padded, columns, axis=2)
        weights = masked_weights[:, block_start:block_stop]
        term = jnp.einsum("ijasd,asdb->ijab", picked, weights, preferred_element_type=jnp.float32)
        ladder = term if ladder is None else ladder + term
    arrived_ladder = lax.all_to_all(
        lax.all_to_all(ladder, "pair", split_axis=1, concat_axis=0, tiled=True),
        "virt",
        split_axis=3,
        concat_axis=2,
        tiled=True,
    )
    partner = jnp.transpose(arrived_ladder, (1, 0, 3, 2))
    occupied_own = lax.dynamic_slice_in_dim(eps_occ, first_row, own_rows)
    virtual_own = lax.dynamic_slice_in_dim(eps_virt, first_tile, own_tiles)
    denominator = (
        occupied_own[:, None, None, None]
        + eps_occ[None, :, None, None]
        - virtual_own[None, None, :, None]
        - eps_virt[None, None, None, :]
    )
    return ((ladder + partner) / denominator).astype(jnp.bfloat16)


def greet_all(pairs, virts):
    count = pairs * virts
    me = lax.axis_index("pair") * virts + lax.axis_index("virt")
    barrier = pltpu.get_barrier_semaphore()

    def greet(d, _):
        t = lax.rem(me + d, count)
        pl.semaphore_signal(
            barrier, inc=1, device_id=(t // virts, lax.rem(t, virts)), device_id_type=MESH
        )
        return 0

    lax.fori_loop(1, count, greet, 0)
    pl.semaphore_wait(barrier, count - 1)


def turn_tiles(block, picked, first):
    tall, held = block.shape[0], block.shape[1]

    def turn(x, _):
        rows = pl.ds(pl.multiple_of(x * 16, 16), 16)
        for c in range(0, held, 16):
            picked[pl.ds(first + c, 16), rows, :] = jnp.swapaxes(block[rows, pl.ds(c, 16), :], 0, 1)
        return 0

    lax.fori_loop(0, tall // 16, turn, 0)


def pack(pairs, mine, codes, scales):
    held, wide = codes.shape[2], codes.shape[3]
    duos = codes.shape[1]
    half = wide // 2
    low = lax.broadcasted_iota(jnp.int32, (held, wide), 1) < half
    low_row = low[:1]

    def one(p, _):
        for m in range(duos):
            tiles, sizes = [], []
            for e in range(2):
                spot = pl.ds(pl.multiple_of((p * 2 * duos + 2 * m + e) * held, 8), held)
                tile = mine[spot, :]
                top = jnp.maximum(jnp.max(jnp.abs(tile), axis=0, keepdims=True), 1e-30)
                tiles.append(jnp.round(tile * (TOP / top)))
                sizes.append(top / TOP)
            for v in range(2):
                moved = [
                    x if v == e else pltpu.roll(x, half, 1) for e, x in enumerate(tiles)
                ]
                code = jnp.where(low, moved[0], moved[1])
                codes[2 * p + v, m] = code.astype(jnp.int32).astype(jnp.int16)
                turned = [
                    x if v == e else pltpu.roll(x, half, 1) for e, x in enumerate(sizes)
                ]
                scales[2 * p + v, pl.ds(m, 1), :] = jnp.where(low_row, turned[0], turned[1])
        return 0

    lax.fori_loop(0, pairs, one, 0)


def meet(level, low, mine, partner, dtype):
    return ((mine + partner) / (level - low)).astype(dtype)


def spread(virt_row, table):
    table[...] = jnp.broadcast_to(virt_row[...], table.shape).T


def fused_kernel(pairs, virts, *refs):
    tiles, counts, occupied, amplitudes, weights, virt_row = refs[:6]
    part, last, arrived, sizes, codes_far, scales_far = refs[6:12]
    own, other, picked, ladder, codes, scales, got_codes, got_sizes, results, table = refs[12:22]
    own_sem, swap_send, swap_recv, hop, send, recv, send_s, recv_s, out_sem, last_sem = refs[22:]
    r, k = pl.program_id(0), pl.program_id(1)
    rows, steps = pl.num_programs(0), pl.num_programs(1)
    chunks, others, held, depth = amplitudes.shape
    block, slots, _, wide = weights.shape
    count = pairs * virts
    p, v = lax.axis_index("pair"), lax.axis_index("virt")
    me = p * virts + v
    duos = codes.shape[1]
    early = chunks - 1

    def own_copy(x):
        return pltpu.make_async_copy(amplitudes.at[x], own, own_sem)

    def swap(x):
        return pltpu.make_async_remote_copy(
            src_ref=amplitudes.at[x],
            dst_ref=other.at[x],
            send_sem=swap_send.at[x],
            recv_sem=swap_recv.at[x],
            device_id=(p, 1 - v),
            device_id_type=MESH,
        )

    def send_to(x, q, w):
        for source, land, sent, got in (
            (codes_far, arrived, send, recv),
            (scales_far, sizes, send_s, recv_s),
        ):
            pltpu.make_async_remote_copy(
                src_ref=source.at[x, q * virts + w],
                dst_ref=land.at[x, me],
                send_sem=sent.at[x],
                recv_sem=got.at[x],
                device_id=(q, w),
                device_id_type=MESH,
            ).start()

    def send_near(x):
        def begin(d, _):
            send_to(x, lax.rem(p + d, pairs), v)
            return 0

        lax.fori_loop(1, pairs, begin, 0)
        pltpu.make_async_copy(codes_far.at[x, me], arrived.at[x, me], recv.at[x]).start()
        pltpu.make_async_copy(scales_far.at[x, me], sizes.at[x, me], recv_s.at[x]).start()

    def send_across(x):
        def begin(d, _):
            send_to(x, lax.rem(p + d, pairs), 1 - v)
            return 0

        lax.fori_loop(0, pairs, begin, 0)

    @pl.when((r == 0) & (k == 0))
    def _():
        own_copy(0).start()
        greet_all(pairs, virts)
        for x in range(chunks):
            swap(x).start()
        picked[2 * held] = jnp.zeros((others, depth), picked.dtype)
        spread(virt_row, table)

    @pl.when(k == 0)
    def _():
        own_copy(r).wait()
        turn_tiles(own, picked, 0)
        swap(r).wait_recv()
        turn_tiles(other.at[r], picked, held)

        @pl.when(r + 1 < rows)
        def _():
            own_copy(r + 1).start()

    @pl.when((k == 0) & (r == rows - 1))
    def _():
        def begin(x, _):
            send_across(x)
            return 0

        lax.fori_loop(0, early, begin, 0)

    for s in range(block):
        a = k * block + s
        live = counts[a]
        parts = []
        for x in range(slots):
            place = lax.rem(tiles[x, a] - v * held + 2 * held, 2 * held)
            parts.append(picked[jnp.where(x < live, place, 2 * held)])
        ladder[r, pl.ds(a, others, stride=held), :] = jnp.dot(
            jnp.concatenate(parts, axis=1),
            weights[s].reshape(slots * depth, wide),
            preferred_element_type=jnp.float32,
        )

    @pl.when(k == steps - 1)
    def _():
        pack(pairs, ladder.at[r], codes, scales)
        hops = (
            pltpu.make_async_copy(codes, codes_far.at[r], hop.at[0]),
            pltpu.make_async_copy(scales, scales_far.at[r], hop.at[1]),
        )
        for copy in hops:
            copy.start()
        for copy in hops:
            copy.wait()
        send_near(r)

    @pl.when((r == rows - 1) & (k == steps - 1))
    def _():
        send_across(early)
        low = table[pl.ds(pl.multiple_of(v * held, 8), held), :] + virt_row[...]

        def keep(q):
            j = q * chunks + early
            rows_of = pl.ds(pl.multiple_of(j * held, 8), held)
            return pltpu.make_async_copy(ladder.at[:, rows_of], last.at[:, q], last_sem.at[q])

        for q in range(pairs):
            keep(q).start()

        def result(n):
            slot = lax.rem(n, 2)
            j = lax.rem(n, pairs) * early + n // pairs
            return pltpu.make_async_copy(results.at[slot], part.at[:, j], out_sem.at[slot])

        def fetch(c):
            pltpu.make_async_copy(arrived.at[c], arrived.at[c], recv.at[c]).wait()
            pltpu.make_async_copy(sizes.at[c], sizes.at[c], recv_s.at[c]).wait()

        def combine(n, _):
            c, q = n // pairs, lax.rem(n, pairs)
            slot = lax.rem(n, 2)

            @pl.when(q == 0)
            def _():
                fetch(c)
                grab = (
                    pltpu.make_async_copy(arrived.at[c], got_codes, hop.at[0]),
                    pltpu.make_async_copy(sizes.at[c], got_sizes, hop.at[1]),
                )
                for copy in grab:
                    copy.start()
                for copy in grab:
                    copy.wait()

            @pl.when(n >= 2)
            def _():
                result(n - 2).wait()

            j = q * chunks + c
            for m in range(duos):
                tile = jnp.concatenate(
                    [
                        got_codes[2 * q + x, m].astype(jnp.float32)
                        * got_sizes[2 * q + x, pl.ds(m, 1), :]
                        for x in range(virts)
                    ],
                    axis=0,
                )
                turned = tile.T
                for e in range(2):
                    i = 2 * m + e
                    mine = ladder[i, pl.ds(pl.multiple_of(j * held, 8), held), :]
                    level = occupied[p * chunks + i] + occupied[j]
                    partner = turned[e * held : (e + 1) * held]
                    results[slot, i] = meet(level, low, mine, partner, results.dtype)
            result(n).start()
            return 0

        total = early * pairs
        lax.fori_loop(0, total, combine, 0)
        result(total - 2).wait()
        result(total - 1).wait()
        for q in range(pairs):
            keep(q).wait()
        for x in range(chunks):
            swap(x).wait_send()
            most = pl.ds(0, count - 1)
            pltpu.make_async_copy(codes_far.at[x, most], codes_far.at[x, most], send.at[x]).wait()
            pltpu.make_async_copy(scales_far.at[x, most], scales_far.at[x, most], send_s.at[x]).wait()
        fetch(early)


def finish_kernel(occupied, part, last, codes, sizes, virt_row, out, table):
    q = pl.program_id(0)
    chunks, _, held, wide = last.shape
    early = part.shape[1]
    virts, duos = codes.shape[1], codes.shape[2]
    p, v = lax.axis_index("pair"), lax.axis_index("virt")

    @pl.when(q == 0)
    def _():
        spread(virt_row, table)

    low = table[pl.ds(pl.multiple_of(v * held, 8), held), :] + virt_row[...]
    for i in range(chunks):
        for c in range(early):
            out[i, c] = part[i, c]
    for m in range(duos):
        tile = jnp.concatenate(
            [codes[0, x, m].astype(jnp.float32) * sizes[0, x, m : m + 1, :] for x in range(virts)],
            axis=0,
        )
        turned = tile.T
        for e in range(2):
            i = 2 * m + e
            level = occupied[p * chunks + i] + occupied[q * chunks + early]
            partner = turned[e * held : (e + 1) * held]
            out[i, early] = meet(level, low, last[i, 0], partner, out.dtype)


def per_device(amplitudes, integrals, cd_tiles, tile_counts, eps_occ, eps_virt):
    pairs, virts = lax.axis_size("pair"), lax.axis_size("virt")
    rows, others, held, depth = amplitudes.shape
    slots, wide = integrals.shape[1], integrals.shape[3]
    fits = virts == 2 and held % 16 == 0 and rows % 2 == 0 and rows <= 16 and others % 16 == 0
    fits = fits and wide == 2 * held and wide == 128 and held % STEP == 0
    if not fits:
        return general_device(amplitudes, integrals, cd_tiles, tile_counts, eps_occ, eps_virt)
    count = pairs * virts
    duos = rows // 2
    steps = held // STEP
    anywhere = pl.BlockSpec(memory_space=pl.ANY)
    vmem = pl.BlockSpec(memory_space=pltpu.VMEM)
    code_shape = (count, duos, held, wide)
    scale_shape = (count, 8, wide)
    flops = 2 * rows * others * held * slots * depth * wide
    virt_row = eps_virt.reshape(1, wide)
    dma = pltpu.SemaphoreType.DMA
    part, last, arrived, sizes, _, _ = pl.pallas_call(
        functools.partial(fused_kernel, pairs, virts),
        grid_spec=pltpu.PrefetchScalarGridSpec(
            num_scalar_prefetch=3,
            grid=(rows, steps),
            in_specs=[
                anywhere,
                pl.BlockSpec((STEP, slots, depth, wide), lambda r, k, *_: (k, 0, 0, 0)),
                vmem,
            ],
            out_specs=[anywhere] * 6,
            scratch_shapes=[
                pltpu.VMEM((others, held, depth), amplitudes.dtype),
                pltpu.VMEM((rows, others, held, depth), amplitudes.dtype),
                pltpu.VMEM((2 * held + 1, others, depth), amplitudes.dtype),
                pltpu.VMEM((rows, others * held, wide), jnp.float32),
                pltpu.VMEM(code_shape, jnp.int16),
                pltpu.VMEM(scale_shape, jnp.float32),
                pltpu.VMEM(code_shape, jnp.int16),
                pltpu.VMEM(scale_shape, jnp.float32),
                pltpu.VMEM((2, rows, held, wide), jnp.bfloat16),
                pltpu.VMEM((wide, wide), jnp.float32),
                dma,
                dma((rows,)),
                dma((rows,)),
                dma((2,)),
                dma((rows,)),
                dma((rows,)),
                dma((rows,)),
                dma((rows,)),
                dma((2,)),
                dma((pairs,)),
            ],
        ),
        out_shape=[
            jax.ShapeDtypeStruct((rows, others - pairs, held, wide), jnp.bfloat16),
            jax.ShapeDtypeStruct((rows, pairs, held, wide), jnp.float32),
            jax.ShapeDtypeStruct((rows,) + code_shape, jnp.int16),
            jax.ShapeDtypeStruct((rows,) + scale_shape, jnp.float32),
            jax.ShapeDtypeStruct((rows,) + code_shape, jnp.int16),
            jax.ShapeDtypeStruct((rows,) + scale_shape, jnp.float32),
        ],
        cost_estimate=pl.CostEstimate(
            flops=flops, bytes_accessed=2 * rows * integrals.size, transcendentals=0
        ),
        compiler_params=pltpu.CompilerParams(
            vmem_limit_bytes=60 * 2**20, collective_id=0, has_side_effects=True
        ),
        name="ladder",
    )(cd_tiles.T, tile_counts, eps_occ, amplitudes, integrals, virt_row)
    final = rows - 1
    return pl.pallas_call(
        finish_kernel,
        grid=(pairs,),
        in_specs=[
            pl.BlockSpec(memory_space=pltpu.SMEM),
            pl.BlockSpec((rows, final, held, wide), lambda q: (0, q, 0, 0)),
            pl.BlockSpec((rows, 1, held, wide), lambda q: (0, q, 0, 0)),
            pl.BlockSpec((1, virts, duos, held, wide), lambda q: (final, q, 0, 0, 0)),
            pl.BlockSpec((1, virts, 8, wide), lambda q: (final, q, 0, 0)),
            vmem,
        ],
        out_specs=pl.BlockSpec((rows, rows, held, wide), lambda q: (0, q, 0, 0)),
        out_shape=jax.ShapeDtypeStruct(amplitudes.shape[:3] + (wide,), jnp.bfloat16),
        scratch_shapes=[pltpu.VMEM((wide, wide), jnp.float32)],
        name="finish",
    )(eps_occ, part, last, arrived, sizes, virt_row)


def solution(mesh):
    in_specs = (
        P("pair", None, "virt", None),
        P("virt", None, None, None),
        P("virt", None),
        P("virt"),
        P(),
        P(),
    )
    out_specs = P("pair", None, "virt", None)
    return jax.shard_map(
        per_device, mesh=mesh, in_specs=in_specs, out_specs=out_specs, check_vma=False
    )
```

```python
import functools

import jax
import jax.numpy as jnp
from jax import lax
from jax.experimental import pallas as pl
from jax.experimental.pallas import tpu as pltpu
from jax.sharding import PartitionSpec as P

MESH = pl.DeviceIdType.MESH
STEP = 8
PASS = 2
TOP = 32700.0
LN2 = 0.6931471805599453


def extended(cells, sides, width):
    for axis, dim in sides:
        count = lax.axis_size(axis)
        ends = count - 1
        head = lax.slice_in_dim(cells, 0, width, axis=dim)
        tail = lax.slice_in_dim(cells, cells.shape[dim] - width, cells.shape[dim], axis=dim)
        cells = jnp.concatenate(
            [
                lax.ppermute(tail, axis, [(i, (i + 1) % count) for i in range(ends)]),
                cells,
                lax.ppermute(head, axis, [((i + 1) % count, i) for i in range(ends)]),
            ],
            axis=dim,
        )
    return cells


def general_device(amplitudes, integrals, cd_tiles, tile_counts, eps_occ, eps_virt):
    own_rows = amplitudes.shape[0]
    own_tiles = amplitudes.shape[2]
    slot_count = integrals.shape[1]
    first_tile = lax.axis_index("virt") * own_tiles
    first_row = lax.axis_index("pair") * own_rows
    local_tiles = cd_tiles - first_tile + own_tiles
    slot_ids = lax.broadcasted_iota(jnp.int32, cd_tiles.shape, 1)
    kept_slots = (slot_ids < tile_counts[:, None]).astype(jnp.bfloat16)
    masked_weights = integrals * kept_slots[:, :, None, None]
    padded = extended(amplitudes, (("virt", 2),), own_tiles)
    block_width = min(4, slot_count)
    ladder = None
    for block_start in range(0, slot_count, block_width):
        block_stop = min(block_start + block_width, slot_count)
        columns = local_tiles[:, block_start:block_stop]
        picked = jnp.take(padded, columns, axis=2)
        weights = masked_weights[:, block_start:block_stop]
        term = jnp.einsum("ijasd,asdb->ijab", picked, weights, preferred_element_type=jnp.float32)
        ladder = term if ladder is None else ladder + term
    arrived_ladder = lax.all_to_all(
        lax.all_to_all(ladder, "pair", split_axis=1, concat_axis=0, tiled=True),
        "virt",
        split_axis=3,
        concat_axis=2,
        tiled=True,
    )
    partner = jnp.transpose(arrived_ladder, (1, 0, 3, 2))
    occupied_own = lax.dynamic_slice_in_dim(eps_occ, first_row, own_rows)
    virtual_own = lax.dynamic_slice_in_dim(eps_virt, first_tile, own_tiles)
    denominator = (
        occupied_own[:, None, None, None]
        + eps_occ[None, :, None, None]
        - virtual_own[None, None, :, None]
        - eps_virt[None, None, None, :]
    )
    return ((ladder + partner) / denominator).astype(jnp.bfloat16)


def greet_all(pairs, virts):
    count = pairs * virts
    me = lax.axis_index("pair") * virts + lax.axis_index("virt")
    barrier = pltpu.get_barrier_semaphore()

    def greet(d, _):
        t = lax.rem(me + d, count)
        pl.semaphore_signal(
            barrier, inc=1, device_id=(t // virts, lax.rem(t, virts)), device_id_type=MESH
        )
        return 0

    lax.fori_loop(1, count, greet, 0)
    pl.semaphore_wait(barrier, count - 1)


def turn_tiles(block, picked, first, above):
    tall, held = block.shape[0], block.shape[1]

    def turn(x, _):
        rows = pl.ds(pl.multiple_of(x * 16, 16), 16)
        below = pl.ds(pl.multiple_of(above + x * 16, 16), 16)
        for c in range(0, held, 16):
            picked[pl.ds(first + c, 16), below, :] = jnp.swapaxes(block[rows, pl.ds(c, 16), :], 0, 1)
        return 0

    lax.fori_loop(0, tall // 16, turn, 0)


def power(exponent):
    return jnp.exp(exponent * LN2)


def pack(pairs, mine, codes):
    wide = codes.shape[2]
    tail = codes.shape[1] % 16
    held = wide // 2
    duos = codes.shape[1] // held
    half = wide // 2
    low = lax.broadcasted_iota(jnp.int32, (held, wide), 1) < half
    low_row = low[:1]
    spots = lax.broadcasted_iota(jnp.int32, (tail, wide), 0)

    def swing(values, v):
        return [x if v == e else pltpu.roll(x, half, 1) for e, x in enumerate(values)]

    def one(p, _):
        notes = [jnp.zeros((tail, wide), jnp.float32)] * 2
        for m in range(duos):
            tiles, sizes = [], []
            for e in range(2):
                spot = pl.ds(pl.multiple_of((p * 2 * duos + 2 * m + e) * held, 8), held)
                tile = mine[spot, :]
                top = jnp.maximum(jnp.max(jnp.abs(tile), axis=0, keepdims=True), 1e-30)
                size = jnp.ceil(jnp.log(top) * (1 / LN2))
                tiles.append(jnp.round(tile * (TOP * power(-size))))
                sizes.append(size)
            for v in range(2):
                code = jnp.where(low, *swing(tiles, v))
                codes[2 * p + v, pl.ds(m * held, held), :] = code.astype(jnp.int32).astype(jnp.int16)
                notes[v] = jnp.where(spots == m, jnp.where(low_row, *swing(sizes, v)), notes[v])
        for v in range(2):
            last = pl.ds(duos * held, tail)
            codes[2 * p + v, last, :] = notes[v].astype(jnp.int32).astype(jnp.int16)
        return 0

    lax.fori_loop(0, pairs, one, 0)


def decode(codes, m, held, steps):
    return codes[m * held : (m + 1) * held].astype(jnp.float32) * steps[m : m + 1, :]


def meet(level, low, mine, partner, dtype):
    return ((mine + partner) / (level - low)).astype(dtype)


def spread(virt_row, table):
    table[...] = jnp.broadcast_to(virt_row[...], table.shape).T


def fused_kernel(pairs, virts, *refs):
    tiles, counts, occupied, amplitudes, weights, virt_row = refs[:6]
    part, last, arrived, codes_far = refs[6:10]
    own, other, picked, ladder, codes, got_codes, results, table = refs[10:18]
    own_sem, swap_send, swap_recv, hop, send, recv, out_sem, last_sem = refs[18:]
    g, k = pl.program_id(0), pl.program_id(1)
    passes, steps = pl.num_programs(0), pl.num_programs(1)
    chunks, others, held, depth = amplitudes.shape
    block, slots, _, wide = weights.shape
    count = pairs * virts
    p, v = lax.axis_index("pair"), lax.axis_index("virt")
    me = p * virts + v
    duos = chunks // 2
    early = chunks - 1
    strides = 4

    def own_copy(x):
        return pltpu.make_async_copy(amplitudes.at[pl.ds(x * PASS, PASS)], own, own_sem)

    def swap(x):
        return pltpu.make_async_remote_copy(
            src_ref=amplitudes.at[x],
            dst_ref=other.at[x],
            send_sem=swap_send.at[x],
            recv_sem=swap_recv.at[x],
            device_id=(p, 1 - v),
            device_id_type=MESH,
        )

    def send_to(x, q, w):
        pltpu.make_async_remote_copy(
            src_ref=codes_far.at[x, q * virts + w],
            dst_ref=arrived.at[x, me],
            send_sem=send.at[x],
            recv_sem=recv.at[x],
            device_id=(q, w),
            device_id_type=MESH,
        ).start()

    def ahead(n):
        return lax.rem(n + p, strides) * (pairs // strides) + n // strides

    def send_near(x):
        def begin(n, _):
            d = ahead(n)

            @pl.when(d > 0)
            def _():
                send_to(x, lax.rem(p + d, pairs), v)

            return 0

        lax.fori_loop(0, pairs, begin, 0)
        pltpu.make_async_copy(codes_far.at[x, me], arrived.at[x, me], recv.at[x]).start()

    def send_across(x):
        def begin(d, _):
            send_to(x, lax.rem(p + ahead(d), pairs), 1 - v)
            return 0

        lax.fori_loop(0, pairs, begin, 0)

    @pl.when((g == 0) & (k == 0))
    def _():
        own_copy(0).start()
        greet_all(pairs, virts)
        for x in range(chunks):
            swap(x).start()
        picked[2 * held] = jnp.zeros((PASS * others, depth), picked.dtype)
        spread(virt_row, table)

    @pl.when(k == 0)
    def _():
        own_copy(g).wait()
        for u in range(PASS):
            turn_tiles(own.at[u], picked, 0, u * others)
        for u in range(PASS):
            swap(g * PASS + u).wait_recv()
            turn_tiles(other.at[g * PASS + u], picked, held, u * others)

        @pl.when(g + 1 < passes)
        def _():
            own_copy(g + 1).start()

    @pl.when((k == 0) & (g == passes - 1))
    def _():
        def begin(x, _):
            send_across(x)
            return 0

        lax.fori_loop(0, chunks - PASS, begin, 0)

    for s in range(block):
        a = k * block + s
        live = counts[a]
        parts = []
        for x in range(slots):
            place = lax.rem(tiles[x, a] - v * held + 2 * held, 2 * held)
            parts.append(picked[jnp.where(x < live, place, 2 * held)])
        ladder[g, pl.ds(a, PASS * others, stride=held), :] = jnp.dot(
            jnp.concatenate(parts, axis=1),
            weights[s].reshape(slots * depth, wide),
            preferred_element_type=jnp.float32,
        )

    @pl.when(k == steps - 1)
    def _():
        def away(u, _):
            x = g * PASS + u
            rows = pl.ds(pl.multiple_of(u * others * held, 8), others * held)
            pack(pairs, ladder.at[g, rows], codes)
            copy = pltpu.make_async_copy(codes, codes_far.at[x], hop)
            copy.start()
            copy.wait()
            send_near(x)

            @pl.when(g == passes - 1)
            def _():
                send_across(x)

            return 0

        lax.fori_loop(0, PASS, away, 0)

    @pl.when((g == passes - 1) & (k == steps - 1))
    def _():
        low = table[pl.ds(pl.multiple_of(v * held, 8), held), :] + virt_row[...]

        def spot(u, j):
            return pl.ds(pl.multiple_of((u * others + j) * held, 8), held)

        def keep(u, q):
            here = ladder.at[:, spot(u, q * chunks + early)]
            return pltpu.make_async_copy(here, last.at[:, u, q], last_sem.at[u, q])

        for q in range(pairs):
            for u in range(PASS):
                keep(u, q).start()

        def result(n):
            slot = lax.rem(n, 2)
            j = lax.rem(n, pairs) * early + n // pairs
            return pltpu.make_async_copy(results.at[slot], part.at[:, j], out_sem.at[slot])

        def fetch(c):
            pltpu.make_async_copy(arrived.at[c], arrived.at[c], recv.at[c]).wait()

        def combine(n, _):
            c, q = n // pairs, lax.rem(n, pairs)
            slot = lax.rem(n, 2)

            @pl.when(q == 0)
            def _():
                fetch(c)
                copy = pltpu.make_async_copy(arrived.at[c], got_codes, hop)
                copy.start()
                copy.wait()

            @pl.when(n >= 2)
            def _():
                result(n - 2).wait()

            j = q * chunks + c
            seen = [got_codes[virts * q + x] for x in range(virts)]
            worth = [power(x[duos * held :].astype(jnp.float32)) * (1 / TOP) for x in seen]
            for m in range(duos):
                tile = jnp.concatenate(
                    [decode(x, m, held, y) for x, y in zip(seen, worth)], axis=0
                )
                turned = tile.T
                for e in range(2):
                    i = 2 * m + e
                    mine = ladder[i // PASS, spot(i % PASS, j), :]
                    level = occupied[p * chunks + i] + occupied[j]
                    partner = turned[e * held : (e + 1) * held]
                    results[slot, i] = meet(level, low, mine, partner, results.dtype)
            result(n).start()
            return 0

        total = early * pairs
        lax.fori_loop(0, total, combine, 0)
        result(total - 2).wait()
        result(total - 1).wait()
        for q in range(pairs):
            for u in range(PASS):
                keep(u, q).wait()
        for x in range(chunks):
            swap(x).wait_send()
            most = pl.ds(0, count - 1)
            pltpu.make_async_copy(codes_far.at[x, most], codes_far.at[x, most], send.at[x]).wait()
        fetch(early)


def finish_kernel(occupied, part, last, codes, virt_row, out, table):
    q = pl.program_id(0)
    chunks, _, held, wide = last.shape
    early = part.shape[1]
    virts, duos = codes.shape[1], chunks // 2
    p, v = lax.axis_index("pair"), lax.axis_index("virt")

    @pl.when(q == 0)
    def _():
        spread(virt_row, table)

    low = table[pl.ds(pl.multiple_of(v * held, 8), held), :] + virt_row[...]
    for i in range(chunks):
        for c in range(early):
            out[i, c] = part[i, c]
    seen = [codes[0, x] for x in range(virts)]
    worth = [power(x[duos * held :].astype(jnp.float32)) * (1 / TOP) for x in seen]
    for m in range(duos):
        tile = jnp.concatenate([decode(x, m, held, y) for x, y in zip(seen, worth)], axis=0)
        turned = tile.T
        for e in range(2):
            i = 2 * m + e
            level = occupied[p * chunks + i] + occupied[q * chunks + early]
            partner = turned[e * held : (e + 1) * held]
            out[i, early] = meet(level, low, last[i, 0], partner, out.dtype)


def per_device(amplitudes, integrals, cd_tiles, tile_counts, eps_occ, eps_virt):
    pairs, virts = lax.axis_size("pair"), lax.axis_size("virt")
    rows, others, held, depth = amplitudes.shape
    slots, wide = integrals.shape[1], integrals.shape[3]
    fits = virts == 2 and held % 16 == 0 and rows % PASS == 0 and rows % 2 == 0 and rows <= 16 and pairs % 4 == 0 and others % 16 == 0
    fits = fits and wide == 2 * held and wide == 128 and held % STEP == 0
    if not fits:
        return general_device(amplitudes, integrals, cd_tiles, tile_counts, eps_occ, eps_virt)
    count = pairs * virts
    duos = rows // 2
    steps = held // STEP
    anywhere = pl.BlockSpec(memory_space=pl.ANY)
    vmem = pl.BlockSpec(memory_space=pltpu.VMEM)
    code_shape = (count, duos * held + 8, wide)
    flops = 2 * rows * others * held * slots * depth * wide
    virt_row = eps_virt.reshape(1, wide)
    dma = pltpu.SemaphoreType.DMA
    part, last, arrived, _ = pl.pallas_call(
        functools.partial(fused_kernel, pairs, virts),
        grid_spec=pltpu.PrefetchScalarGridSpec(
            num_scalar_prefetch=3,
            grid=(rows // PASS, steps),
            in_specs=[
                anywhere,
                pl.BlockSpec((STEP, slots, depth, wide), lambda r, k, *_: (k, 0, 0, 0)),
                vmem,
            ],
            out_specs=[anywhere] * 4,
            scratch_shapes=[
                pltpu.VMEM((PASS, others, held, depth), amplitudes.dtype),
                pltpu.VMEM((rows, others, held, depth), amplitudes.dtype),
                pltpu.VMEM((2 * held + 1, PASS * others, depth), amplitudes.dtype),
                pltpu.VMEM((rows // PASS, PASS * others * held, wide), jnp.float32),
                pltpu.VMEM(code_shape, jnp.int16),
                pltpu.VMEM(code_shape, jnp.int16),
                pltpu.VMEM((2, rows, held, wide), jnp.bfloat16),
                pltpu.VMEM((wide, wide), jnp.float32),
                dma,
                dma((rows,)),
                dma((rows,)),
                dma,
                dma((rows,)),
                dma((rows,)),
                dma((2,)),
                dma((PASS, pairs)),
            ],
        ),
        out_shape=[
            jax.ShapeDtypeStruct((rows, others - pairs, held, wide), jnp.bfloat16),
            jax.ShapeDtypeStruct((rows // PASS, PASS, pairs, held, wide), jnp.float32),
            jax.ShapeDtypeStruct((rows,) + code_shape, jnp.int16),
            jax.ShapeDtypeStruct((rows,) + code_shape, jnp.int16),
        ],
        cost_estimate=pl.CostEstimate(
            flops=flops, bytes_accessed=2 * rows // PASS * integrals.size, transcendentals=0
        ),
        compiler_params=pltpu.CompilerParams(
            vmem_limit_bytes=60 * 2**20, collective_id=0, has_side_effects=True
        ),
        name="ladder",
    )(cd_tiles.T, tile_counts, eps_occ, amplitudes, integrals, virt_row)
    final = rows - 1
    return pl.pallas_call(
        finish_kernel,
        grid=(pairs,),
        in_specs=[
            pl.BlockSpec(memory_space=pltpu.SMEM),
            pl.BlockSpec((rows, final, held, wide), lambda q: (0, q, 0, 0)),
            pl.BlockSpec((rows, 1, held, wide), lambda q: (0, q, 0, 0)),
            pl.BlockSpec((1, virts) + code_shape[1:], lambda q: (final, q, 0, 0)),
            vmem,
        ],
        out_specs=pl.BlockSpec((rows, rows, held, wide), lambda q: (0, q, 0, 0)),
        out_shape=jax.ShapeDtypeStruct(amplitudes.shape[:3] + (wide,), jnp.bfloat16),
        scratch_shapes=[pltpu.VMEM((wide, wide), jnp.float32)],
        name="finish",
    )(eps_occ, part, last.reshape(rows, pairs, held, wide), arrived, virt_row)


def solution(mesh):
    in_specs = (
        P("pair", None, "virt", None),
        P("virt", None, None, None),
        P("virt", None),
        P("virt"),
        P(),
        P(),
    )
    out_specs = P("pair", None, "virt", None)
    return jax.shard_map(
        per_device, mesh=mesh, in_specs=in_specs, out_specs=out_specs, check_vma=False
    )
```

```python
import functools

import jax
import jax.numpy as jnp
from jax import lax
from jax.experimental import pallas as pl
from jax.experimental.pallas import tpu as pltpu
from jax.sharding import PartitionSpec as P

MESH = pl.DeviceIdType.MESH
NOTES = 8
STEP = 8
TOP = 32700.0
LN2 = 0.6931471805599453


def extended(cells, sides, width):
    for axis, dim in sides:
        count = lax.axis_size(axis)
        ends = count - 1
        head = lax.slice_in_dim(cells, 0, width, axis=dim)
        tail = lax.slice_in_dim(cells, cells.shape[dim] - width, cells.shape[dim], axis=dim)
        cells = jnp.concatenate(
            [
                lax.ppermute(tail, axis, [(i, (i + 1) % count) for i in range(ends)]),
                cells,
                lax.ppermute(head, axis, [((i + 1) % count, i) for i in range(ends)]),
            ],
            axis=dim,
        )
    return cells


def general_device(amplitudes, integrals, cd_tiles, tile_counts, eps_occ, eps_virt):
    own_rows = amplitudes.shape[0]
    own_tiles = amplitudes.shape[2]
    slot_count = integrals.shape[1]
    first_tile = lax.axis_index("virt") * own_tiles
    first_row = lax.axis_index("pair") * own_rows
    local_tiles = cd_tiles - first_tile + own_tiles
    slot_ids = lax.broadcasted_iota(jnp.int32, cd_tiles.shape, 1)
    kept_slots = (slot_ids < tile_counts[:, None]).astype(jnp.bfloat16)
    masked_weights = integrals * kept_slots[:, :, None, None]
    padded = extended(amplitudes, (("virt", 2),), own_tiles)
    block_width = min(4, slot_count)
    ladder = None
    for block_start in range(0, slot_count, block_width):
        block_stop = min(block_start + block_width, slot_count)
        columns = local_tiles[:, block_start:block_stop]
        picked = jnp.take(padded, columns, axis=2)
        weights = masked_weights[:, block_start:block_stop]
        term = jnp.einsum("ijasd,asdb->ijab", picked, weights, preferred_element_type=jnp.float32)
        ladder = term if ladder is None else ladder + term
    arrived_ladder = lax.all_to_all(
        lax.all_to_all(ladder, "pair", split_axis=1, concat_axis=0, tiled=True),
        "virt",
        split_axis=3,
        concat_axis=2,
        tiled=True,
    )
    partner = jnp.transpose(arrived_ladder, (1, 0, 3, 2))
    occupied_own = lax.dynamic_slice_in_dim(eps_occ, first_row, own_rows)
    virtual_own = lax.dynamic_slice_in_dim(eps_virt, first_tile, own_tiles)
    denominator = (
        occupied_own[:, None, None, None]
        + eps_occ[None, :, None, None]
        - virtual_own[None, None, :, None]
        - eps_virt[None, None, None, :]
    )
    return ((ladder + partner) / denominator).astype(jnp.bfloat16)


def greet_all(pairs, virts):
    count = pairs * virts
    me = lax.axis_index("pair") * virts + lax.axis_index("virt")
    barrier = pltpu.get_barrier_semaphore()

    def greet(d, _):
        t = lax.rem(me + d, count)
        pl.semaphore_signal(
            barrier, inc=1, device_id=(t // virts, lax.rem(t, virts)), device_id_type=MESH
        )
        return 0

    lax.fori_loop(1, count, greet, 0)
    pl.semaphore_wait(barrier, count - 1)


def turn_tiles(block, picked, first, start, size):
    tall, held = block.shape[0], block.shape[2]

    def turn(x, _):
        rows = pl.ds(pl.multiple_of(x * tall, 16), tall)
        for c in range(0, held, 16):
            picked[pl.ds(first + c, 16), rows, :] = jnp.swapaxes(block[:, x, pl.ds(c, 16), :], 0, 1)
        return 0

    lax.fori_loop(start, start + size, turn, 0)


def power(exponent):
    return jnp.exp(exponent * LN2)


def pack(pairs, mine, codes, start, size):
    wide = codes.shape[2]
    half = held = wide // 2
    duos = size // 2
    low = lax.broadcasted_iota(jnp.int32, (held, wide), 1) < half
    low_row = low[:1]
    spots = lax.broadcasted_iota(jnp.int32, (NOTES, wide), 0)

    def swing(values, v):
        return [x if v == e else pltpu.roll(x, half, 1) for e, x in enumerate(values)]

    def one(p, _):
        notes = [jnp.zeros((NOTES, wide), jnp.float32)] * 2
        for m in range(duos):
            tiles, sizes = [], []
            for e in range(2):
                at = (start + 2 * m + e) * pairs + p
                tile = mine[pl.ds(pl.multiple_of(at * held, 8), held), :]
                top = jnp.maximum(jnp.max(jnp.abs(tile), axis=0, keepdims=True), 1e-30)
                grade = jnp.ceil(jnp.log(top) * (1 / LN2))
                tiles.append(jnp.round(tile * (TOP * power(-grade))))
                sizes.append(grade)
            for v in range(2):
                code = jnp.where(low, *swing(tiles, v))
                codes[2 * p + v, pl.ds(m * held, held), :] = code.astype(jnp.int32).astype(jnp.int16)
                notes[v] = jnp.where(spots == m, jnp.where(low_row, *swing(sizes, v)), notes[v])
        for v in range(2):
            last = pl.ds(duos * held, NOTES)
            codes[2 * p + v, last, :] = notes[v].astype(jnp.int32).astype(jnp.int16)
        return 0

    lax.fori_loop(0, pairs, one, 0)


def decode(codes, m, held, steps):
    return codes[m * held : (m + 1) * held].astype(jnp.float32) * steps[m : m + 1, :]


def meet(level, low, mine, partner, dtype):
    return ((mine + partner) / (level - low)).astype(dtype)


def partners(seen, duos, held):
    tops = [power(x[duos * held : duos * held + NOTES].astype(jnp.float32)) * (1 / TOP) for x in seen]
    for m in range(duos):
        tile = jnp.concatenate([decode(x, m, held, y) for x, y in zip(seen, tops)], axis=0)
        turned = tile.T
        yield 2 * m, turned[:held]
        yield 2 * m + 1, turned[held:]


def fused_kernel(pairs, virts, cut, *refs):
    tiles, counts, occupied, amplitudes, weights, virt_row = refs[:6]
    part, last, arrived, codes_far = refs[6:10]
    own, other, picked, ladder, codes, got_codes, results, table = refs[10:18]
    own_sem, swap_send, swap_recv, hop, send, recv, out_sem, last_sem = refs[18:]
    g, k = pl.program_id(0), pl.program_id(1)
    steps = pl.num_programs(1)
    rows, _, _, held, depth = amplitudes.shape
    block, slots, _, wide = weights.shape
    others = pairs * rows
    count = pairs * virts
    p, v = lax.axis_index("pair"), lax.axis_index("virt")
    me = p * virts + v
    final = rows - 1
    strides = 4
    chunks = [(x, x, 0, rows) for x in range(final)]
    chunks += [(final, final, 0, cut), (rows, final, cut, rows - cut)]

    def own_copy(i):
        return pltpu.make_async_copy(amplitudes.at[i], own, own_sem)

    def swap(x, i, start, size):
        some = pl.ds(start, size)
        return pltpu.make_async_remote_copy(
            src_ref=amplitudes.at[i, :, some],
            dst_ref=other.at[i, :, some],
            send_sem=swap_send.at[x],
            recv_sem=swap_recv.at[x],
            device_id=(p, 1 - v),
            device_id_type=MESH,
        )

    def tall(size):
        return pl.ds(0, size // 2 * held + NOTES)

    def ahead(n):
        return lax.rem(n + p, strides) * (pairs // strides) + n // strides

    def send_to(x, size, q, w):
        pltpu.make_async_remote_copy(
            src_ref=codes_far.at[x, q * virts + w, tall(size)],
            dst_ref=arrived.at[x, me, tall(size)],
            send_sem=send.at[x],
            recv_sem=recv.at[x],
            device_id=(q, w),
            device_id_type=MESH,
        ).start()

    def send_near(x, size):
        def begin(n, _):
            d = ahead(n)

            @pl.when(d > 0)
            def _():
                send_to(x, size, lax.rem(p + d, pairs), v)

            return 0

        lax.fori_loop(0, pairs, begin, 0)
        pltpu.make_async_copy(
            codes_far.at[x, me, tall(size)], arrived.at[x, me, tall(size)], recv.at[x]
        ).start()

    def send_across(x, size):
        def begin(n, _):
            send_to(x, size, lax.rem(p + ahead(n), pairs), 1 - v)
            return 0

        lax.fori_loop(0, pairs, begin, 0)

    @pl.when((g == 0) & (k == 0))
    def _():
        own_copy(0).start()
        greet_all(pairs, virts)
        for chunk in chunks:
            swap(*chunk).start()
        picked[2 * held] = jnp.zeros((others, depth), picked.dtype)
        table[...] = jnp.broadcast_to(virt_row[...], table.shape).T

    def load(x, i, start, size):
        @pl.when(k == 0)
        def _():
            if not start:
                own_copy(i).wait()
                turn_tiles(own, picked, 0, 0, rows)

                @pl.when(i < final)
                def _():
                    own_copy(i + 1).start()

            swap(x, i, start, size).wait_recv()
            turn_tiles(other.at[i], picked, held, start, size)

    def multiply(i, start, size):
        span = pl.ds(start * pairs, size * pairs)
        for s in range(block):
            a = k * block + s
            live = counts[a]
            parts = []
            for x in range(slots):
                place = lax.rem(tiles[x, a] - v * held + 2 * held, 2 * held)
                parts.append(picked[jnp.where(x < live, place, 2 * held), span])
            first = start * pairs * held + a
            ladder[i, pl.ds(first, size * pairs, stride=held), :] = jnp.dot(
                jnp.concatenate(parts, axis=1),
                weights[s].reshape(slots * depth, wide),
                preferred_element_type=jnp.float32,
            )

    def leave(x, i, start, size):
        pack(pairs, ladder.at[i], codes, start, size)
        copy = pltpu.make_async_copy(codes.at[:, tall(size)], codes_far.at[x, :, tall(size)], hop)
        copy.start()
        copy.wait()
        send_near(x, size)

    @pl.when(g < final)
    def _():
        load(g, g, 0, rows)
        multiply(g, 0, rows)

        @pl.when(k == steps - 1)
        def _():
            leave(g, g, 0, rows)

    @pl.when(g == final)
    def _():
        load(*chunks[final])

        @pl.when(k == 0)
        def _():
            def begin(x, _):
                send_across(x, rows)
                return 0

            lax.fori_loop(0, final, begin, 0)

        multiply(final, 0, cut)

        @pl.when(k == steps - 1)
        def _():
            leave(*chunks[final])
            send_across(final, cut)

    def combine_all():
        low = table[pl.ds(pl.multiple_of(v * held, 8), held), :] + virt_row[...]
        tail = pl.ds(final * pairs * held, pairs * held)
        keep = pltpu.make_async_copy(ladder.at[pl.ds(cut, rows - cut), tail], last, last_sem)
        keep.start()

        def result(n, size):
            slot, some = lax.rem(n, 2), pl.ds(0, size)
            j = lax.rem(n, pairs) * rows + n // pairs
            return pltpu.make_async_copy(results.at[slot, some], part.at[some, j], out_sem.at[slot])

        def fetch(x, size):
            land = arrived.at[x, :, tall(size)]
            pltpu.make_async_copy(land, land, recv.at[x]).wait()

        def pull(x, size):
            fetch(x, size)
            copy = pltpu.make_async_copy(
                arrived.at[x, :, tall(size)], got_codes.at[:, tall(size)], hop
            )
            copy.start()
            copy.wait()

        def combine(n, size):
            c, q = n // pairs, lax.rem(n, pairs)
            slot = lax.rem(n, 2)
            j = q * rows + c
            seen = [got_codes[virts * q + x] for x in range(virts)]
            for i, partner in partners(seen, size // 2, held):
                mine = ladder[i, pl.ds(pl.multiple_of((c * pairs + q) * held, 8), held), :]
                level = occupied[p * rows + i] + occupied[j]
                results[slot, i] = meet(level, low, mine, partner, results.dtype)
            result(n, size).start()

        def whole(n, _):
            @pl.when(lax.rem(n, pairs) == 0)
            def _():
                pull(n // pairs, rows)

            @pl.when(n >= 2)
            def _():
                result(n - 2, rows).wait()

            combine(n, rows)
            return 0

        def some(n, _):
            @pl.when(n >= 2)
            def _():
                result(full + n - 2, cut).wait()

            combine(full + n, cut)
            return 0

        full = final * pairs
        lax.fori_loop(0, full, whole, 0)
        for n in (2, 1):
            result(full - n, rows).wait()
        pull(final, cut)
        lax.fori_loop(0, pairs, some, 0)
        for n in (2, 1):
            result(full + pairs - n, cut).wait()
        keep.wait()
        for chunk in chunks:
            x, _, _, size = chunk
            swap(*chunk).wait_send()
            sent = codes_far.at[x, pl.ds(0, count - 1), tall(size)]
            pltpu.make_async_copy(sent, sent, send.at[x]).wait()
        fetch(rows, rows - cut)

    @pl.when(g == rows)
    def _():
        load(*chunks[rows])
        multiply(final, cut, rows - cut)

        @pl.when(k == steps - 1)
        def _():
            leave(*chunks[rows])
            send_across(rows, rows - cut)
            combine_all()


def finish_kernel(occupied, part, last, codes, virt_row, out, table):
    q = pl.program_id(0)
    rows, held = part.shape[0], part.shape[2]
    left, virts = last.shape[0], codes.shape[1]
    cut, final = rows - left, rows - 1
    p, v = lax.axis_index("pair"), lax.axis_index("virt")

    @pl.when(q == 0)
    def _():
        table[...] = jnp.broadcast_to(virt_row[...], table.shape).T

    low = table[pl.ds(pl.multiple_of(v * held, 8), held), :] + virt_row[...]
    for i in range(rows):
        for c in range(rows if i < cut else final):
            out[i, c] = part[i, c]
    seen = [codes[0, x] for x in range(virts)]
    for e, partner in partners(seen, left // 2, held):
        level = occupied[p * rows + cut + e] + occupied[q * rows + final]
        out[cut + e, final] = meet(level, low, last[e, 0], partner, out.dtype)


def per_device(amplitudes, integrals, cd_tiles, tile_counts, eps_occ, eps_virt):
    pairs, virts = lax.axis_size("pair"), lax.axis_size("virt")
    rows, others, held, depth = amplitudes.shape
    slots, wide = integrals.shape[1], integrals.shape[3]
    fits = virts == 2 and held % 16 == 0 and rows % 2 == 0 and 4 <= rows <= 16
    fits = fits and pairs % 16 == 0 and wide == 2 * held and wide == 128 and held % STEP == 0
    if not fits:
        return general_device(amplitudes, integrals, cd_tiles, tile_counts, eps_occ, eps_virt)
    count = pairs * virts
    steps = held // STEP
    cut = rows - 2
    left = rows - cut
    anywhere = pl.BlockSpec(memory_space=pl.ANY)
    vmem = pl.BlockSpec(memory_space=pltpu.VMEM)
    code_shape = (count, rows // 2 * held + NOTES, wide)
    flops = 2 * rows * others * held * slots * depth * wide
    virt_row = eps_virt.reshape(1, wide)
    dma = pltpu.SemaphoreType.DMA
    parted = amplitudes.reshape(rows, pairs, rows, held, depth)
    part, last, arrived, _ = pl.pallas_call(
        functools.partial(fused_kernel, pairs, virts, cut),
        grid_spec=pltpu.PrefetchScalarGridSpec(
            num_scalar_prefetch=3,
            grid=(rows + 1, steps),
            in_specs=[
                anywhere,
                pl.BlockSpec((STEP, slots, depth, wide), lambda g, k, *_: (k, 0, 0, 0)),
                vmem,
            ],
            out_specs=[anywhere] * 4,
            scratch_shapes=[
                pltpu.VMEM((pairs, rows, held, depth), amplitudes.dtype),
                pltpu.VMEM((rows, pairs, rows, held, depth), amplitudes.dtype),
                pltpu.VMEM((2 * held + 1, others, depth), amplitudes.dtype),
                pltpu.VMEM((rows, others * held, wide), jnp.float32),
                pltpu.VMEM(code_shape, jnp.int16),
                pltpu.VMEM(code_shape, jnp.int16),
                pltpu.VMEM((2, rows, held, wide), jnp.bfloat16),
                pltpu.VMEM((wide, wide), jnp.float32),
                dma,
                dma((rows + 1,)),
                dma((rows + 1,)),
                dma,
                dma((rows + 1,)),
                dma((rows + 1,)),
                dma((2,)),
                dma,
            ],
        ),
        out_shape=[
            jax.ShapeDtypeStruct((rows, others, held, wide), jnp.bfloat16),
            jax.ShapeDtypeStruct((left, pairs * held, wide), jnp.float32),
            jax.ShapeDtypeStruct((rows + 1,) + code_shape, jnp.int16),
            jax.ShapeDtypeStruct((rows + 1,) + code_shape, jnp.int16),
        ],
        cost_estimate=pl.CostEstimate(
            flops=flops, bytes_accessed=2 * (rows + 1) * integrals.size, transcendentals=0
        ),
        compiler_params=pltpu.CompilerParams(
            vmem_limit_bytes=60 * 2**20, collective_id=0, has_side_effects=True
        ),
        name="ladder",
    )(cd_tiles.T, tile_counts, eps_occ, parted, integrals, virt_row)
    few = left // 2 * held + NOTES
    return pl.pallas_call(
        finish_kernel,
        grid=(pairs,),
        in_specs=[
            pl.BlockSpec(memory_space=pltpu.SMEM),
            pl.BlockSpec((rows, rows, held, wide), lambda q: (0, q, 0, 0)),
            pl.BlockSpec((left, 1, held, wide), lambda q: (0, q, 0, 0)),
            pl.BlockSpec((1, virts, few, wide), lambda q: (rows, q, 0, 0)),
            vmem,
        ],
        out_specs=pl.BlockSpec((rows, rows, held, wide), lambda q: (0, q, 0, 0)),
        out_shape=jax.ShapeDtypeStruct(amplitudes.shape[:3] + (wide,), jnp.bfloat16),
        scratch_shapes=[pltpu.VMEM((wide, wide), jnp.float32)],
        name="finish",
    )(eps_occ, part, last.reshape(left, pairs, held, wide), arrived, virt_row)


def solution(mesh):
    in_specs = (
        P("pair", None, "virt", None),
        P("virt", None, None, None),
        P("virt", None),
        P("virt"),
        P(),
        P(),
    )
    out_specs = P("pair", None, "virt", None)
    return jax.shard_map(
        per_device, mesh=mesh, in_specs=in_specs, out_specs=out_specs, check_vma=False
    )
```

```python
import functools

import jax
import jax.numpy as jnp
from jax import lax
from jax.experimental import pallas as pl
from jax.experimental.pallas import tpu as pltpu
from jax.sharding import PartitionSpec as P

MESH = pl.DeviceIdType.MESH
NOTES = 8
BESIDE = 3
STEP = 8
TOP = 32700.0
LN2 = 0.6931471805599453


def extended(cells, sides, width):
    for axis, dim in sides:
        count = lax.axis_size(axis)
        ends = count - 1
        head = lax.slice_in_dim(cells, 0, width, axis=dim)
        tail = lax.slice_in_dim(cells, cells.shape[dim] - width, cells.shape[dim], axis=dim)
        cells = jnp.concatenate(
            [
                lax.ppermute(tail, axis, [(i, (i + 1) % count) for i in range(ends)]),
                cells,
                lax.ppermute(head, axis, [((i + 1) % count, i) for i in range(ends)]),
            ],
            axis=dim,
        )
    return cells


def general_device(amplitudes, integrals, cd_tiles, tile_counts, eps_occ, eps_virt):
    own_rows = amplitudes.shape[0]
    own_tiles = amplitudes.shape[2]
    slot_count = integrals.shape[1]
    first_tile = lax.axis_index("virt") * own_tiles
    first_row = lax.axis_index("pair") * own_rows
    local_tiles = cd_tiles - first_tile + own_tiles
    slot_ids = lax.broadcasted_iota(jnp.int32, cd_tiles.shape, 1)
    kept_slots = (slot_ids < tile_counts[:, None]).astype(jnp.bfloat16)
    masked_weights = integrals * kept_slots[:, :, None, None]
    padded = extended(amplitudes, (("virt", 2),), own_tiles)
    block_width = min(4, slot_count)
    ladder = None
    for block_start in range(0, slot_count, block_width):
        block_stop = min(block_start + block_width, slot_count)
        columns = local_tiles[:, block_start:block_stop]
        picked = jnp.take(padded, columns, axis=2)
        weights = masked_weights[:, block_start:block_stop]
        term = jnp.einsum("ijasd,asdb->ijab", picked, weights, preferred_element_type=jnp.float32)
        ladder = term if ladder is None else ladder + term
    arrived_ladder = lax.all_to_all(
        lax.all_to_all(ladder, "pair", split_axis=1, concat_axis=0, tiled=True),
        "virt",
        split_axis=3,
        concat_axis=2,
        tiled=True,
    )
    partner = jnp.transpose(arrived_ladder, (1, 0, 3, 2))
    occupied_own = lax.dynamic_slice_in_dim(eps_occ, first_row, own_rows)
    virtual_own = lax.dynamic_slice_in_dim(eps_virt, first_tile, own_tiles)
    denominator = (
        occupied_own[:, None, None, None]
        + eps_occ[None, :, None, None]
        - virtual_own[None, None, :, None]
        - eps_virt[None, None, None, :]
    )
    return ((ladder + partner) / denominator).astype(jnp.bfloat16)


def greet_all(pairs, virts):
    count = pairs * virts
    me = lax.axis_index("pair") * virts + lax.axis_index("virt")
    barrier = pltpu.get_barrier_semaphore()

    def greet(d, _):
        t = lax.rem(me + d, count)
        pl.semaphore_signal(
            barrier, inc=1, device_id=(t // virts, lax.rem(t, virts)), device_id_type=MESH
        )
        return 0

    lax.fori_loop(1, count, greet, 0)
    pl.semaphore_wait(barrier, count - 1)


def turn_tiles(block, picked, first, start, size):
    tall, held = block.shape[0], block.shape[2]

    def turn(x, _):
        rows = pl.ds(pl.multiple_of(x * tall, 16), tall)
        for c in range(0, held, 16):
            picked[pl.ds(first + c, 16), rows, :] = jnp.swapaxes(block[:, x, pl.ds(c, 16), :], 0, 1)
        return 0

    lax.fori_loop(start, start + size, turn, 0)


def power(exponent):
    return jnp.exp(exponent * LN2)


def pack(pairs, mine, codes, start, size):
    wide = codes.shape[2]
    half = held = wide // 2
    duos = size // 2
    low = lax.broadcasted_iota(jnp.int32, (held, wide), 1) < half
    low_row = low[:1]
    spots = lax.broadcasted_iota(jnp.int32, (NOTES, wide), 0)

    def swing(values, v):
        return [x if v == e else pltpu.roll(x, half, 1) for e, x in enumerate(values)]

    def one(p, _):
        notes = [jnp.zeros((NOTES, wide), jnp.float32)] * 2
        for m in range(duos):
            tiles, sizes = [], []
            for e in range(2):
                at = (start + 2 * m + e) * pairs + p
                tile = mine[pl.ds(pl.multiple_of(at * held, 8), held), :]
                top = jnp.maximum(jnp.max(jnp.abs(tile), axis=0, keepdims=True), 1e-30)
                grade = jnp.ceil(jnp.log(top) * (1 / LN2))
                tiles.append(jnp.round(tile * (TOP * power(-grade))))
                sizes.append(grade)
            for v in range(2):
                code = jnp.where(low, *swing(tiles, v))
                codes[2 * p + v, pl.ds(m * held, held), :] = code.astype(jnp.int32).astype(jnp.int16)
                notes[v] = jnp.where(spots == m, jnp.where(low_row, *swing(sizes, v)), notes[v])
        for v in range(2):
            last = pl.ds(duos * held, NOTES)
            codes[2 * p + v, last, :] = notes[v].astype(jnp.int32).astype(jnp.int16)
        return 0

    lax.fori_loop(0, pairs, one, 0)


def decode(codes, m, held, steps):
    return codes[m * held : (m + 1) * held].astype(jnp.float32) * steps[m : m + 1, :]


def meet(level, low, mine, partner, dtype):
    return ((mine + partner) / (level - low)).astype(dtype)


def partners(seen, duos, held):
    tops = [power(x[duos * held : duos * held + NOTES].astype(jnp.float32)) * (1 / TOP) for x in seen]
    for m in range(duos):
        tile = jnp.concatenate([decode(x, m, held, y) for x, y in zip(seen, tops)], axis=0)
        turned = tile.T
        yield 2 * m, turned[:held]
        yield 2 * m + 1, turned[held:]


def fused_kernel(pairs, virts, cut, *refs):
    tiles, counts, occupied, amplitudes, weights, virt_row = refs[:6]
    part, last, arrived, codes_far = refs[6:10]
    own, other, picked, ladder, codes, got_codes, results, table = refs[10:18]
    own_sem, swap_send, swap_recv, hop, send, recv, out_sem, last_sem = refs[18:]
    g, k = pl.program_id(0), pl.program_id(1)
    steps = pl.num_programs(1)
    weights_steps = amplitudes.shape[3] // weights.shape[0]
    rows, _, _, held, depth = amplitudes.shape
    block, slots, _, wide = weights.shape
    others = pairs * rows
    count = pairs * virts
    p, v = lax.axis_index("pair"), lax.axis_index("virt")
    me = p * virts + v
    final = rows - 1
    strides = 4
    chunks = [(x, x, 0, rows) for x in range(final)]
    chunks += [(final, final, 0, cut), (rows, final, cut, rows - cut)]

    def own_copy(i):
        return pltpu.make_async_copy(amplitudes.at[i], own, own_sem)

    def swap(x, i, start, size):
        some = pl.ds(start, size)
        return pltpu.make_async_remote_copy(
            src_ref=amplitudes.at[i, :, some],
            dst_ref=other.at[i, :, some],
            send_sem=swap_send.at[x],
            recv_sem=swap_recv.at[x],
            device_id=(p, 1 - v),
            device_id_type=MESH,
        )

    def tall(size):
        return pl.ds(0, size // 2 * held + NOTES)

    def ahead(n):
        return lax.rem(n + p, strides) * (pairs // strides) + n // strides

    def send_to(x, size, q, w):
        pltpu.make_async_remote_copy(
            src_ref=codes_far.at[x, q * virts + w, tall(size)],
            dst_ref=arrived.at[x, me, tall(size)],
            send_sem=send.at[x],
            recv_sem=recv.at[x],
            device_id=(q, w),
            device_id_type=MESH,
        ).start()

    def send_near(x, size):
        def begin(n, _):
            d = ahead(n)

            @pl.when(d > 0)
            def _():
                send_to(x, size, lax.rem(p + d, pairs), v)

            return 0

        lax.fori_loop(0, pairs, begin, 0)
        pltpu.make_async_copy(
            codes_far.at[x, me, tall(size)], arrived.at[x, me, tall(size)], recv.at[x]
        ).start()

    def send_across(x, size):
        def begin(n, _):
            send_to(x, size, lax.rem(p + ahead(n), pairs), 1 - v)
            return 0

        lax.fori_loop(0, pairs, begin, 0)

    @pl.when((g == 0) & (k == 0))
    def _():
        own_copy(0).start()
        greet_all(pairs, virts)
        for chunk in chunks:
            swap(*chunk).start()
        picked[2 * held] = jnp.zeros((others, depth), picked.dtype)
        table[...] = jnp.broadcast_to(virt_row[...], table.shape).T

    def load(x, i, start, size):
        @pl.when(k == 0)
        def _():
            if not start:
                own_copy(i).wait()
                turn_tiles(own, picked, 0, 0, rows)

                @pl.when(i < final)
                def _():
                    own_copy(i + 1).start()

            swap(x, i, start, size).wait_recv()
            turn_tiles(other.at[i], picked, held, start, size)

    def multiply(i, start, size):
        span = pl.ds(start * pairs, size * pairs)
        for s in range(block):
            a = k * block + s
            live = counts[a]
            parts = []
            for x in range(slots):
                place = lax.rem(tiles[x, a] - v * held + 2 * held, 2 * held)
                parts.append(picked[jnp.where(x < live, place, 2 * held), span])
            first = start * pairs * held + a
            ladder[i, pl.ds(first, size * pairs, stride=held), :] = jnp.dot(
                jnp.concatenate(parts, axis=1),
                weights[s].reshape(slots * depth, wide),
                preferred_element_type=jnp.float32,
            )

    def leave(x, i, start, size):
        pack(pairs, ladder.at[i], codes, start, size)
        copy = pltpu.make_async_copy(codes.at[:, tall(size)], codes_far.at[x, :, tall(size)], hop)
        copy.start()
        copy.wait()
        send_near(x, size)

    @pl.when(g < final)
    def _():
        load(g, g, 0, rows)
        multiply(g, 0, rows)

        @pl.when(k == steps - 1)
        def _():
            leave(g, g, 0, rows)

    @pl.when(g == final)
    def _():
        load(*chunks[final])

        @pl.when(k == 0)
        def _():
            def begin(x, _):
                send_across(x, rows)
                return 0

            lax.fori_loop(0, final, begin, 0)

        multiply(final, 0, cut)

        @pl.when(k == steps - 1)
        def _():
            leave(*chunks[final])
            send_across(final, cut)

    def result(n, size):
        slot, some = lax.rem(n, 2), pl.ds(0, size)
        j = lax.rem(n, pairs) * rows + n // pairs
        return pltpu.make_async_copy(results.at[slot, some], part.at[some, j], out_sem.at[slot])

    def fetch(x, size):
        land = arrived.at[x, :, tall(size)]
        pltpu.make_async_copy(land, land, recv.at[x]).wait()

    def pull(x, size):
        fetch(x, size)
        copy = pltpu.make_async_copy(arrived.at[x, :, tall(size)], got_codes.at[:, tall(size)], hop)
        copy.start()
        copy.wait()

    def combine(n, size):
        low = table[pl.ds(pl.multiple_of(v * held, 8), held), :] + virt_row[...]
        c, q = n // pairs, lax.rem(n, pairs)
        slot = lax.rem(n, 2)
        j = q * rows + c
        seen = [got_codes[virts * q + x] for x in range(virts)]
        for i, partner in partners(seen, size // 2, held):
            mine = ladder[i, pl.ds(pl.multiple_of((c * pairs + q) * held, 8), held), :]
            level = occupied[p * rows + i] + occupied[j]
            results[slot, i] = meet(level, low, mine, partner, results.dtype)
        result(n, size).start()

    def whole(n, _):
        @pl.when(lax.rem(n, pairs) == 0)
        def _():
            pull(n // pairs, rows)

        @pl.when(n >= 2)
        def _():
            result(n - 2, rows).wait()

        combine(n, rows)
        return 0

    share = BESIDE * pairs // weights_steps

    def combine_all():
        tail = pl.ds(final * pairs * held, pairs * held)
        keep = pltpu.make_async_copy(ladder.at[pl.ds(cut, rows - cut), tail], last, last_sem)
        keep.start()

        def some(n, _):
            @pl.when(n >= 2)
            def _():
                result(full + n - 2, cut).wait()

            combine(full + n, cut)
            return 0

        full = final * pairs
        lax.fori_loop(share * weights_steps, full, whole, 0)
        for n in (2, 1):
            result(full - n, rows).wait()
        pull(final, cut)
        lax.fori_loop(0, pairs, some, 0)
        for n in (2, 1):
            result(full + pairs - n, cut).wait()
        keep.wait()
        for chunk in chunks:
            x, _, _, size = chunk
            swap(*chunk).wait_send()
            sent = codes_far.at[x, pl.ds(0, count - 1), tall(size)]
            pltpu.make_async_copy(sent, sent, send.at[x]).wait()
        fetch(rows, rows - cut)

    @pl.when(g == rows)
    def _():
        load(*chunks[rows])
        multiply(final, cut, rows - cut)
        lax.fori_loop(k * share, (k + 1) * share, whole, 0)

        @pl.when(k == steps - 1)
        def _():
            leave(*chunks[rows])
            send_across(rows, rows - cut)
            combine_all()


def finish_kernel(occupied, part, last, codes, virt_row, out, table):
    q = pl.program_id(0)
    rows, held = part.shape[0], part.shape[2]
    left, virts = last.shape[0], codes.shape[1]
    cut, final = rows - left, rows - 1
    p, v = lax.axis_index("pair"), lax.axis_index("virt")

    @pl.when(q == 0)
    def _():
        table[...] = jnp.broadcast_to(virt_row[...], table.shape).T

    low = table[pl.ds(pl.multiple_of(v * held, 8), held), :] + virt_row[...]
    for i in range(rows):
        for c in range(rows if i < cut else final):
            out[i, c] = part[i, c]
    seen = [codes[0, x] for x in range(virts)]
    for e, partner in partners(seen, left // 2, held):
        level = occupied[p * rows + cut + e] + occupied[q * rows + final]
        out[cut + e, final] = meet(level, low, last[e, 0], partner, out.dtype)


def per_device(amplitudes, integrals, cd_tiles, tile_counts, eps_occ, eps_virt):
    pairs, virts = lax.axis_size("pair"), lax.axis_size("virt")
    rows, others, held, depth = amplitudes.shape
    slots, wide = integrals.shape[1], integrals.shape[3]
    fits = virts == 2 and held % 16 == 0 and rows % 2 == 0 and BESIDE < rows - 2 and rows <= 16
    fits = fits and pairs % 16 == 0 and wide == 2 * held and wide == 128 and held % STEP == 0
    if not fits:
        return general_device(amplitudes, integrals, cd_tiles, tile_counts, eps_occ, eps_virt)
    count = pairs * virts
    steps = held // STEP
    cut = rows - 2
    left = rows - cut
    anywhere = pl.BlockSpec(memory_space=pl.ANY)
    vmem = pl.BlockSpec(memory_space=pltpu.VMEM)
    code_shape = (count, rows // 2 * held + NOTES, wide)
    flops = 2 * rows * others * held * slots * depth * wide
    virt_row = eps_virt.reshape(1, wide)
    dma = pltpu.SemaphoreType.DMA
    parted = amplitudes.reshape(rows, pairs, rows, held, depth)
    part, last, arrived, _ = pl.pallas_call(
        functools.partial(fused_kernel, pairs, virts, cut),
        grid_spec=pltpu.PrefetchScalarGridSpec(
            num_scalar_prefetch=3,
            grid=(rows + 1, steps),
            in_specs=[
                anywhere,
                pl.BlockSpec((STEP, slots, depth, wide), lambda g, k, *_: (k, 0, 0, 0)),
                vmem,
            ],
            out_specs=[anywhere] * 4,
            scratch_shapes=[
                pltpu.VMEM((pairs, rows, held, depth), amplitudes.dtype),
                pltpu.VMEM((rows, pairs, rows, held, depth), amplitudes.dtype),
                pltpu.VMEM((2 * held + 1, others, depth), amplitudes.dtype),
                pltpu.VMEM((rows, others * held, wide), jnp.float32),
                pltpu.VMEM(code_shape, jnp.int16),
                pltpu.VMEM(code_shape, jnp.int16),
                pltpu.VMEM((2, rows, held, wide), jnp.bfloat16),
                pltpu.VMEM((wide, wide), jnp.float32),
                dma,
                dma((rows + 1,)),
                dma((rows + 1,)),
                dma,
                dma((rows + 1,)),
                dma((rows + 1,)),
                dma((2,)),
                dma,
            ],
        ),
        out_shape=[
            jax.ShapeDtypeStruct((rows, others, held, wide), jnp.bfloat16),
            jax.ShapeDtypeStruct((left, pairs * held, wide), jnp.float32),
            jax.ShapeDtypeStruct((rows + 1,) + code_shape, jnp.int16),
            jax.ShapeDtypeStruct((rows + 1,) + code_shape, jnp.int16),
        ],
        cost_estimate=pl.CostEstimate(
            flops=flops, bytes_accessed=2 * (rows + 1) * integrals.size, transcendentals=0
        ),
        compiler_params=pltpu.CompilerParams(
            vmem_limit_bytes=60 * 2**20, collective_id=0, has_side_effects=True
        ),
        name="ladder",
    )(cd_tiles.T, tile_counts, eps_occ, parted, integrals, virt_row)
    few = left // 2 * held + NOTES
    return pl.pallas_call(
        finish_kernel,
        grid=(pairs,),
        in_specs=[
            pl.BlockSpec(memory_space=pltpu.SMEM),
            pl.BlockSpec((rows, rows, held, wide), lambda q: (0, q, 0, 0)),
            pl.BlockSpec((left, 1, held, wide), lambda q: (0, q, 0, 0)),
            pl.BlockSpec((1, virts, few, wide), lambda q: (rows, q, 0, 0)),
            vmem,
        ],
        out_specs=pl.BlockSpec((rows, rows, held, wide), lambda q: (0, q, 0, 0)),
        out_shape=jax.ShapeDtypeStruct(amplitudes.shape[:3] + (wide,), jnp.bfloat16),
        scratch_shapes=[pltpu.VMEM((wide, wide), jnp.float32)],
        name="finish",
    )(eps_occ, part, last.reshape(left, pairs, held, wide), arrived, virt_row)


def solution(mesh):
    in_specs = (
        P("pair", None, "virt", None),
        P("virt", None, None, None),
        P("virt", None),
        P("virt"),
        P(),
        P(),
    )
    out_specs = P("pair", None, "virt", None)
    return jax.shard_map(
        per_device, mesh=mesh, in_specs=in_specs, out_specs=out_specs, check_vma=False
    )
```
